32 devices in a mesh: gx: 4 (over y, x), gy: 8 (over z, core).
Axes of the slice: x: 2, y: 2, z: 4, core: 2. Of those that a mesh axis runs over, the one named last changes fastest.
Arguments:
- source_heat: float32 [160, 64, 1024], P(None, 'gx', 'gy'), may hold values from -8 to 8
- horiz_coef: float32 [160], replicated, may hold values from 0.5 to 4
- face_coef: float32 [161], replicated, may hold values from 0.25 to 4
- column_inverse: float32 [160, 160], replicated, as said below
Outputs:
- pressure: float32 [160, 64, 1024], P(None, 'gx', 'gy')
- true_residual: float32 [160, 64, 1024], P(None, 'gx', 'gy')
The draws below stay inside these ranges and needn't reach their ends.
Inputs may be any that keep to these rules, and one draw needn't show every extreme that they name: `column_inverse`: the inverse of the tridiagonal matrix with diagonal 4 horiz_coef[k] + face_coef[k] + face_coef[k+1] and off-diagonal entries -face_coef[k] between levels k-1 and k.
All inputs are finite; a program needn't handle non-finite values.
Results may differ from the reference program's by a relative error of at most 0.0003.
Values sent between devices are 32-bit elements; how exact they have to be, the bound alone decides.
A program may use at most 64 MiB of HBM per device.

```python
import jax
import jax.numpy as jnp
from jax import lax

NZ = 160
ITERS = 3
NX = 64
NY = 1024


def column_setup(key):
    base = jax.random.fold_in(key, 11)
    key_horiz = jax.random.fold_in(base, 1)
    key_faces = jax.random.fold_in(base, 2)
    horizontal = jnp.exp(jax.random.uniform(key_horiz, (NZ,), jnp.float32, jnp.log(0.5), jnp.log(4.0)))
    face_coef = jnp.exp(jax.random.uniform(key_faces, (NZ + 1,), jnp.float32, jnp.log(0.25), jnp.log(4.0)))
    diagonal = 4.0 * horizontal + face_coef[:-1] + face_coef[1:]
    tridiag = jnp.diag(diagonal) - jnp.diag(face_coef[1:-1], 1) - jnp.diag(face_coef[1:-1], -1)
    inverse = jnp.linalg.solve(tridiag, jnp.eye(NZ, dtype=jnp.float32))
    return (horizontal, face_coef, inverse)


def draw_horiz_coef(key, part):
    return column_setup(key)[0]


def draw_face_coef(key, part):
    return column_setup(key)[1]


def draw_column_inverse(key, part):
    return column_setup(key)[2]


def draw_source_heat(key, part):
    noise_key = jax.random.fold_in(key, 23)
    return jnp.clip(jax.random.normal(noise_key, (NZ, NX, NY), jnp.float32), -8.0, 8.0)


def setup_inputs(seed: int = 0) -> dict:
    streams_of = jax.random.split(jax.random.key(seed), 5)
    return {
        "source_heat": draw_source_heat(jax.random.fold_in(streams_of[4], 71), 0),
        "horiz_coef": draw_horiz_coef(jax.random.fold_in(streams_of[4], 71), 0),
        "face_coef": draw_face_coef(jax.random.fold_in(streams_of[4], 71), 0),
        "column_inverse": draw_column_inverse(jax.random.fold_in(streams_of[4], 71), 0),
    }


def operate(values_in, horizontal, face_coef):
    padded = jnp.pad(values_in, ((0, 0), (1, 1), (1, 1)), mode='wrap')
    beside = padded[:, 2:, 1:-1] + padded[:, :-2, 1:-1] + padded[:, 1:-1, 2:] + padded[:, 1:-1, :-2]
    zero_layer = jnp.zeros_like(values_in[:1])
    upward = jnp.concatenate([values_in[1:], zero_layer], 0)
    downward = jnp.concatenate([zero_layer, values_in[:-1]], 0)
    lower_face = face_coef[:-1][:, None, None]
    upper_face = face_coef[1:][:, None, None]
    return horizontal[:, None, None] * (4.0 * values_in - beside) + upper_face * (values_in - upward) + lower_face * (values_in - downward)

def precondition(values_in, column_inverse):
    layout = values_in.shape
    columns = values_in.reshape(layout[0], -1)
    return jnp.dot(column_inverse, columns, precision=lax.Precision.HIGHEST).reshape(layout)

def reference(source_heat, horiz_coef, face_coef, column_inverse):
    pressure = jnp.zeros_like(source_heat)
    residual = source_heat
    precond = precondition(residual, column_inverse)
    direction = precond
    inner = jnp.sum(residual * precond)
    for iteration in range(ITERS):
        image = operate(direction, horiz_coef, face_coef)
        step_len = inner / jnp.sum(direction * image)
        pressure = pressure + step_len * direction
        residual = residual - step_len * image
        if iteration + 1 < ITERS:
            precond = precondition(residual, column_inverse)
            inner_next = jnp.sum(residual * precond)
            direction = precond + inner_next / inner * direction
            inner = inner_next
    true_residual = source_heat - operate(pressure, horiz_coef, face_coef)
    return (pressure, true_residual)
```

```python
import functools

import jax
import jax.numpy as jnp
from jax import lax
from jax.experimental import pallas as pl
from jax.experimental.pallas import tpu as pltpu
from jax.sharding import PartitionSpec as P

ITERS = 3
MESH = pl.DeviceIdType.MESH
F32 = jnp.float32
BF16 = jnp.bfloat16


def split2(v):
    high = v.astype(BF16)
    low = (v - high.astype(F32)).astype(BF16)
    return high, low


def folded(v):
    return jnp.sum(v.reshape(v.shape[0] // 8, 8, v.shape[1]), axis=0)


def coefficients(m):
    rho, delta, press = [None], [None], []
    inner = m[0]
    one = jnp.ones_like(m[0])
    rho, delta = [one], [one]
    for it in range(ITERS):
        n = len(delta)
        dad = 0.0
        for i in range(n):
            for j in range(n):
                dad = dad + delta[i] * delta[j] * (m[i + j] - m[i + j + 1])
        step = inner / dad
        press = [
            (press[i] if i < len(press) else 0.0) + step * delta[i] for i in range(n)
        ]
        image = [
            (delta[i] if i < n else 0.0) - (delta[i - 1] if i else 0.0)
            for i in range(n + 1)
        ]
        rho = [(rho[i] if i < n else 0.0) - step * image[i] for i in range(n + 1)]
        if it + 1 < ITERS:
            inner_next = 0.0
            for i in range(n + 1):
                for j in range(n + 1):
                    inner_next = inner_next + rho[i] * rho[j] * m[i + j]
            ratio = inner_next / inner
            delta = [
                rho[i] + (ratio * delta[i] if i < n else 0.0) for i in range(n + 1)
            ]
            inner = inner_next
    resid = [
        (press[i] if i < ITERS else 0.0) for i in range(ITERS)
    ]
    resid = (
        [1.0 - press[0]]
        + [press[i - 1] - press[i] for i in range(1, ITERS)]
        + [press[ITERS - 1]]
    )
    return press, resid


def kernel(
    sx, sy, b_hbm, h_ref, m_ref, p_hbm, r_hbm,
    bs, ws, mcat, pack, halo, part, slots_x, mid, slots_y,
    load_sem, store_sem, xs_sem, xr_sem, ys_sem, yr_sem,
    ax_s, ax_r, ay_s, ay_r,
):
    K, X, Y = b_hbm.shape
    G = Y // (2 * X)
    KG = K // G
    ix, iy = lax.axis_index("gx"), lax.axis_index("gy")
    xn, xp = lax.rem(ix + 1, sx), lax.rem(ix + sx - 1, sx)
    yn, yp = lax.rem(iy + 1, sy), lax.rem(iy + sy - 1, sy)

    barrier = pltpu.get_barrier_semaphore()
    for d in range(1, sx):
        pl.semaphore_signal(
            barrier, inc=1, device_id={"gx": lax.rem(ix + d, sx)}, device_id_type=MESH
        )
    for d in range(1, sy):
        pl.semaphore_signal(
            barrier, inc=1, device_id={"gy": lax.rem(iy + d, sy)}, device_id_type=MESH
        )

    order = [0, X - 1] + list(range(1, X - 1))
    loads = {
        x: pltpu.make_async_copy(b_hbm.at[:, x, :], bs.at[0, x], load_sem.at[x])
        for x in order
    }
    for x in order:
        loads[x].start()

    m1, m2 = split2(m_ref[...])
    mcat[...] = jnp.concatenate([m1.astype(F32), m1.astype(F32), m2.astype(F32)], axis=1).astype(BF16)
    rows = lax.broadcasted_iota(jnp.int32, (K, K), 0)
    cols = lax.broadcasted_iota(jnp.int32, (K, K), 1)
    h_col = jnp.sum(jnp.where(rows == cols, h_ref[...], 0.0), axis=1, keepdims=True)
    h_b = jnp.broadcast_to(h_col, (K, Y))
    lane = lax.broadcasted_iota(jnp.int32, (KG, Y), 1)
    lane_full = lax.broadcasted_iota(jnp.int32, (K, Y), 1)

    def matmul(v0, v1):
        h0, l0 = split2(v0)
        h1, l1 = split2(v1)
        high = jnp.concatenate([h0, h1], axis=1)
        low = jnp.concatenate([l0, l1], axis=1)
        stacked = jnp.concatenate([high, low, high], axis=0)
        out = jnp.dot(mcat[...], stacked, preferred_element_type=F32)
        return out[:, :Y], out[:, Y:]

    def packed(j, x, v):
        acc = pack[j]
        for g in range(G):
            shift = lax.rem(2 * X * g + 2 * x, Y)
            turned = pltpu.roll(v[g * KG:(g + 1) * KG], shift, 1)
            here = (lane == shift) | (lane == lax.rem(shift + Y - 1, Y))
            acc = jnp.where(here, turned, acc)
        pack[j] = acc

    def beside(j, x):
        v = ws[j, x + 1]
        c = halo[j]
        turned = jnp.concatenate(
            [
                pltpu.roll(c, lax.rem(2 * Y - 2 * X * g - 2 * x, Y), 1)
                for g in range(G)
            ],
            axis=0,
        )
        left = jnp.where(lane_full == 0, turned, pltpu.roll(v, 1, 1))
        right = jnp.where(lane_full == Y - 1, turned, pltpu.roll(v, Y - 1, 1))
        total = ws[j, x] + ws[j, x + 2] + left + right
        return v, total

    def through_m(j, x0, x1, v0, v1):
        w0, w1 = matmul(v0, v1)
        ws[j, x0 + 1] = w0
        ws[j, x1 + 1] = w1
        packed(j, x0, w0)
        packed(j, x1, w1)
        return folded(v0 * w0 + v1 * w1)

    def level(j, x0, x1):
        w0, s0 = beside(j, x0)
        w1, s1 = beside(j, x1)
        b0, b1 = h_b * s0, h_b * s1
        bs[j + 1, x0] = b0
        bs[j + 1, x1] = b1
        odd = folded(b0 * w0 + b1 * w1)
        even = None
        if j + 1 < ITERS:
            even = through_m(j + 1, x0, x1, b0, b1)
        return odd, even

    def x_copies(j):
        return (
            pltpu.make_async_remote_copy(
                src_ref=ws.at[j, X], dst_ref=ws.at[j, 0],
                send_sem=xs_sem.at[j, 0], recv_sem=xr_sem.at[j, 0],
                device_id={"gx": xn}, device_id_type=MESH,
            ),
            pltpu.make_async_remote_copy(
                src_ref=ws.at[j, 1], dst_ref=ws.at[j, X + 1],
                send_sem=xs_sem.at[j, 1], recv_sem=xr_sem.at[j, 1],
                device_id={"gx": xp}, device_id_type=MESH,
            ),
        )

    def y_copies(j):
        return (
            pltpu.make_async_remote_copy(
                src_ref=pack.at[j], dst_ref=pack.at[ITERS + j],
                send_sem=ys_sem.at[j, 0], recv_sem=yr_sem.at[j, 0],
                device_id={"gy": yn}, device_id_type=MESH,
            ),
            pltpu.make_async_remote_copy(
                src_ref=pack.at[j], dst_ref=pack.at[2 * ITERS + j],
                send_sem=ys_sem.at[j, 1], recv_sem=yr_sem.at[j, 1],
                device_id={"gy": yp}, device_id_type=MESH,
            ),
        )

    zero = jnp.zeros((8, Y), F32)
    moments = [zero] * (2 * ITERS)
    for j in range(ITERS):
        pack[j] = jnp.zeros((KG, Y), F32)

    loads[0].wait()
    loads[X - 1].wait()
    even = through_m(0, 0, X - 1, bs[0, 0], bs[0, X - 1])
    pl.semaphore_wait(barrier, sx - 1 + sy - 1)
    sent_x = [x_copies(0)]
    for copy in sent_x[0]:
        copy.start()
    for x in range(1, X - 1):
        loads[x].wait()

    def first(i, acc):
        x0 = 2 * i + 1
        return acc + through_m(0, x0, x0 + 1, bs[0, x0], bs[0, x0 + 1])

    moments[0] = lax.fori_loop(0, (X - 2) // 2, first, even)
    sent_y = [y_copies(0)]
    for copy in sent_y[0]:
        copy.start()

    for j in range(ITERS):
        for copy in sent_y[j]:
            copy.wait()
        from_left, from_right = pack[ITERS + j], pack[2 * ITERS + j]
        halo[j] = jnp.where(
            lane % 2 == 0, pltpu.roll(from_left, 1, 1), pltpu.roll(from_right, Y - 1, 1)
        )

        def inside(i, acc):
            x0 = 2 * i + 1
            odd, even = level(j, x0, x0 + 1)
            if even is None:
                return (acc[0] + odd,)
            return (acc[0] + odd, acc[1] + even)

        start = (zero,) if j + 1 == ITERS else (zero, zero)
        got = lax.fori_loop(0, (X - 2) // 2, inside, start)
        for copy in sent_x[j]:
            copy.wait()
        odd, even = level(j, 0, X - 1)
        moments[2 * j + 1] = got[0] + odd
        if j + 1 < ITERS:
            moments[2 * j + 2] = got[1] + even
            sent_x.append(x_copies(j + 1))
            for copy in sent_x[j + 1]:
                copy.start()
            sent_y.append(y_copies(j + 1))
            for copy in sent_y[j + 1]:
                copy.start()

    part[...] = jnp.concatenate(
        [jnp.sum(t, axis=0, keepdims=True) for t in moments]
        + [jnp.zeros((8 - 2 * ITERS, Y), F32)],
        axis=0,
    )

    def total_over(axis, me, size, source, slots, send_sem, recv_sem):
        copies = []
        for d in range(1, size):
            copies.append(
                pltpu.make_async_remote_copy(
                    src_ref=source, dst_ref=slots.at[d - 1],
                    send_sem=send_sem.at[d - 1], recv_sem=recv_sem.at[d - 1],
                    device_id={axis: lax.rem(me + d, size)}, device_id_type=MESH,
                )
            )
            copies[-1].start()
        total = source[...]
        for d in range(1, size):
            copies[d - 1].wait()
            total = total + slots[d - 1]
        return total

    mid[...] = total_over("gx", ix, sx, part, slots_x, ax_s, ax_r)
    total = total_over("gy", iy, sy, mid, slots_y, ay_s, ay_r)
    summed = jnp.broadcast_to(jnp.sum(total, axis=1, keepdims=True), (8, Y))
    press, resid = coefficients([summed[i:i + 1] for i in range(2 * ITERS)])

    for x in range(X):
        p = press[0] * ws[0, x + 1]
        r = resid[0] * bs[0, x]
        for j in range(1, ITERS):
            p = p + press[j] * ws[j, x + 1]
        for j in range(1, ITERS + 1):
            r = r + resid[j] * bs[j, x]
        ws[0, x + 1] = p
        bs[0, x] = r
        pltpu.make_async_copy(ws.at[0, x + 1], p_hbm.at[:, x, :], store_sem.at[0, x]).start()
        pltpu.make_async_copy(bs.at[0, x], r_hbm.at[:, x, :], store_sem.at[1, x]).start()
    for x in range(X):
        pltpu.make_async_copy(ws.at[0, x + 1], p_hbm.at[:, x, :], store_sem.at[0, x]).wait()
        pltpu.make_async_copy(bs.at[0, x], r_hbm.at[:, x, :], store_sem.at[1, x]).wait()


def on_device(sx, sy, source_heat, horiz_coef, face_coef, column_inverse):
    K, X, Y = source_heat.shape
    KG = K // (Y // (2 * X))
    any_spec = pl.BlockSpec(memory_space=pl.ANY)
    vmem = pl.BlockSpec(memory_space=pltpu.VMEM)
    dma = pltpu.SemaphoreType.DMA
    out = jax.ShapeDtypeStruct((K, X, Y), F32)
    return pl.pallas_call(
        functools.partial(kernel, sx, sy),
        out_shape=(out, out),
        in_specs=[any_spec, vmem, vmem],
        out_specs=(any_spec, any_spec),
        scratch_shapes=[
            pltpu.VMEM((ITERS + 1, X, K, Y), F32),
            pltpu.VMEM((ITERS, X + 2, K, Y), F32),
            pltpu.VMEM((K, 3 * K), BF16),
            pltpu.VMEM((3 * ITERS, KG, Y), F32),
            pltpu.VMEM((ITERS, KG, Y), F32),
            pltpu.VMEM((8, Y), F32),
            pltpu.VMEM((sx - 1, 8, Y), F32),
            pltpu.VMEM((8, Y), F32),
            pltpu.VMEM((sy - 1, 8, Y), F32),
            dma((X,)),
            dma((2, X)),
            dma((ITERS, 2)),
            dma((ITERS, 2)),
            dma((ITERS, 2)),
            dma((ITERS, 2)),
            dma((sx - 1,)),
            dma((sx - 1,)),
            dma((sy - 1,)),
            dma((sy - 1,)),
        ],
        compiler_params=pltpu.CompilerParams(
            collective_id=0, has_side_effects=True, vmem_limit_bytes=40 << 20
        ),
        name="pcg",
    )(source_heat, horiz_coef.reshape(1, K), column_inverse)


def solution(mesh):
    in_specs = (P(None, "gx", "gy"), P(), P(), P())
    out_specs = (P(None, "gx", "gy"), P(None, "gx", "gy"))
    body = functools.partial(on_device, mesh.shape["gx"], mesh.shape["gy"])
    return jax.shard_map(
        body, mesh=mesh, in_specs=in_specs, out_specs=out_specs, check_vma=False
    )
```

```python
import functools

import jax
import jax.numpy as jnp
from jax import lax
from jax.experimental import pallas as pl
from jax.experimental.pallas import tpu as pltpu
from jax.sharding import PartitionSpec as P

ITERS = 3
MESH = pl.DeviceIdType.MESH
F32 = jnp.float32
BF16 = jnp.bfloat16


def split2(v):
    high = v.astype(BF16)
    low = (v - high.astype(F32)).astype(BF16)
    return high, low


def folded(v):
    return jnp.sum(v.reshape(v.shape[0] // 8, 8, v.shape[1]), axis=0)


def coefficients(m):
    press = []
    inner = m[0]
    one = jnp.ones_like(m[0])
    rho, delta = [one], [one]
    for it in range(ITERS):
        n = len(delta)
        dad = 0.0
        for i in range(n):
            for j in range(n):
                dad = dad + delta[i] * delta[j] * (m[i + j] - m[i + j + 1])
        step = inner / dad
        press = [
            (press[i] if i < len(press) else 0.0) + step * delta[i] for i in range(n)
        ]
        image = [
            (delta[i] if i < n else 0.0) - (delta[i - 1] if i else 0.0)
            for i in range(n + 1)
        ]
        rho = [(rho[i] if i < n else 0.0) - step * image[i] for i in range(n + 1)]
        if it + 1 < ITERS:
            inner_next = 0.0
            for i in range(n + 1):
                for j in range(n + 1):
                    inner_next = inner_next + rho[i] * rho[j] * m[i + j]
            ratio = inner_next / inner
            delta = [
                rho[i] + (ratio * delta[i] if i < n else 0.0) for i in range(n + 1)
            ]
            inner = inner_next
    resid = (
        [1.0 - press[0]]
        + [press[i - 1] - press[i] for i in range(1, ITERS)]
        + [press[ITERS - 1]]
    )
    return press, resid


def kernel(
    sx, sy, b_hbm, h_hbm, m_hbm, bs, ws, coef,
    h_ref, m_ref, mcat, pack, halo, part, slots_x, mid, slots_y,
    load_sem, small_sem, xs_sem, xr_sem, ys_sem, yr_sem,
    ax_s, ax_r, ay_s, ay_r,
):
    K, X, Y = b_hbm.shape
    G = Y // (2 * X)
    KG = K // G
    ix, iy = lax.axis_index("gx"), lax.axis_index("gy")
    xn, xp = lax.rem(ix + 1, sx), lax.rem(ix + sx - 1, sx)
    yn, yp = lax.rem(iy + 1, sy), lax.rem(iy + sy - 1, sy)

    barrier = pltpu.get_barrier_semaphore()
    for d in range(1, sx):
        pl.semaphore_signal(
            barrier, inc=1, device_id={"gx": lax.rem(ix + d, sx)}, device_id_type=MESH
        )
    for d in range(1, sy):
        pl.semaphore_signal(
            barrier, inc=1, device_id={"gy": lax.rem(iy + d, sy)}, device_id_type=MESH
        )

    order = [0, X - 1] + list(range(1, X - 1))
    loads = {
        x: pltpu.make_async_copy(b_hbm.at[:, x, :], bs.at[0, x], load_sem.at[x])
        for x in order
    }
    load_h = pltpu.make_async_copy(h_hbm, h_ref, small_sem.at[0])
    load_m = pltpu.make_async_copy(m_hbm, m_ref, small_sem.at[1])
    load_m.start()
    load_h.start()
    for x in order:
        loads[x].start()
    load_m.wait()
    load_h.wait()

    m1, m2 = split2(m_ref[...])
    mcat[...] = jnp.concatenate([m1.astype(F32), m1.astype(F32), m2.astype(F32)], axis=1).astype(BF16)
    rows = lax.broadcasted_iota(jnp.int32, (K, K), 0)
    cols = lax.broadcasted_iota(jnp.int32, (K, K), 1)
    h_col = jnp.sum(jnp.where(rows == cols, h_ref[...], 0.0), axis=1, keepdims=True)
    h_b = jnp.broadcast_to(h_col, (K, Y))
    lane = lax.broadcasted_iota(jnp.int32, (KG, Y), 1)
    lane_full = lax.broadcasted_iota(jnp.int32, (K, Y), 1)

    def matmul(v0, v1):
        h0, l0 = split2(v0)
        h1, l1 = split2(v1)
        high = jnp.concatenate([h0, h1], axis=1)
        low = jnp.concatenate([l0, l1], axis=1)
        stacked = jnp.concatenate([high, low, high], axis=0)
        out = jnp.dot(mcat[...], stacked, preferred_element_type=F32)
        return out[:, :Y], out[:, Y:]

    def packed(j, x, v):
        acc = pack[j]
        for g in range(G):
            shift = lax.rem(2 * X * g + 2 * x, Y)
            turned = pltpu.roll(v[g * KG:(g + 1) * KG], shift, 1)
            here = (lane == shift) | (lane == lax.rem(shift + Y - 1, Y))
            acc = jnp.where(here, turned, acc)
        pack[j] = acc

    def turned_sum(v):
        return pltpu.roll(v, 1, 1) + pltpu.roll(v, Y - 1, 1)

    def periodic(j, x):
        bs[j + 1, x] = ws[j, x] + ws[j, x + 2] + turned_sum(ws[j, x + 1])

    edge = (lane_full == 0) | (lane_full == Y - 1)

    def beside(j, x):
        c = halo[j]
        turned = jnp.concatenate(
            [
                pltpu.roll(c, lax.rem(2 * Y - 2 * X * g - 2 * x, Y), 1)
                for g in range(G)
            ],
            axis=0,
        )
        return ws[j, x + 1], bs[j + 1, x] + jnp.where(edge, turned, 0.0)

    def through_m(j, x0, x1, v0, v1):
        w0, w1 = matmul(v0, v1)
        ws[j, x0 + 1] = w0
        ws[j, x1 + 1] = w1
        packed(j, x0, w0)
        packed(j, x1, w1)
        return folded(v0 * w0 + v1 * w1)

    def level(j, x0, x1):
        w0, s0 = beside(j, x0)
        w1, s1 = beside(j, x1)
        b0, b1 = h_b * s0, h_b * s1
        bs[j + 1, x0] = b0
        bs[j + 1, x1] = b1
        odd = folded(b0 * w0 + b1 * w1)
        even = None
        if j + 1 < ITERS:
            even = through_m(j + 1, x0, x1, b0, b1)
        return odd, even

    def x_copies(j):
        return (
            pltpu.make_async_remote_copy(
                src_ref=ws.at[j, X], dst_ref=ws.at[j, 0],
                send_sem=xs_sem.at[j, 0], recv_sem=xr_sem.at[j, 0],
                device_id={"gx": xn}, device_id_type=MESH,
            ),
            pltpu.make_async_remote_copy(
                src_ref=ws.at[j, 1], dst_ref=ws.at[j, X + 1],
                send_sem=xs_sem.at[j, 1], recv_sem=xr_sem.at[j, 1],
                device_id={"gx": xp}, device_id_type=MESH,
            ),
        )

    def y_copies(j):
        return (
            pltpu.make_async_remote_copy(
                src_ref=pack.at[j], dst_ref=pack.at[ITERS + j],
                send_sem=ys_sem.at[j, 0], recv_sem=yr_sem.at[j, 0],
                device_id={"gy": yn}, device_id_type=MESH,
            ),
            pltpu.make_async_remote_copy(
                src_ref=pack.at[j], dst_ref=pack.at[2 * ITERS + j],
                send_sem=ys_sem.at[j, 1], recv_sem=yr_sem.at[j, 1],
                device_id={"gy": yp}, device_id_type=MESH,
            ),
        )

    zero = jnp.zeros((8, Y), F32)
    moments = [zero] * (2 * ITERS)
    for j in range(ITERS):
        pack[j] = jnp.zeros((KG, Y), F32)

    loads[0].wait()
    loads[X - 1].wait()
    even = through_m(0, 0, X - 1, bs[0, 0], bs[0, X - 1])

    def first(i, acc):
        x0 = 2 * i + 1
        for x in (x0, x0 + 1):
            pltpu.make_async_copy(b_hbm.at[:, x, :], bs.at[0, x], load_sem.at[x]).wait()
        return acc + through_m(0, x0, x0 + 1, bs[0, x0], bs[0, x0 + 1])

    moments[0] = lax.fori_loop(0, (X - 2) // 2, first, even)
    pl.semaphore_wait(barrier, sx - 1 + sy - 1)
    sent_y = [y_copies(0)]
    for copy in sent_y[0]:
        copy.start()
    sent_x = [x_copies(0)]
    for copy in sent_x[0]:
        copy.start()

    for j in range(ITERS):
        def ahead(i, carry):
            periodic(j, 2 * i + 1)
            periodic(j, 2 * i + 2)
            return carry

        lax.fori_loop(0, (X - 2) // 2, ahead, 0)
        for copy in sent_y[j]:
            copy.wait()
        mine = pack[j]
        from_left, from_right = pack[ITERS + j] - mine, pack[2 * ITERS + j] - mine
        halo[j] = jnp.where(
            lane % 2 == 0, pltpu.roll(from_left, 1, 1), pltpu.roll(from_right, Y - 1, 1)
        )

        def inside(i, acc):
            x0 = 2 * i + 1
            odd, even = level(j, x0, x0 + 1)
            if even is None:
                return (acc[0] + odd,)
            return (acc[0] + odd, acc[1] + even)

        start = (zero,) if j + 1 == ITERS else (zero, zero)
        got = lax.fori_loop(0, (X - 2) // 2, inside, start)
        for copy in sent_x[j]:
            copy.wait()
        periodic(j, 0)
        periodic(j, X - 1)
        odd, even = level(j, 0, X - 1)
        moments[2 * j + 1] = got[0] + odd
        if j + 1 < ITERS:
            moments[2 * j + 2] = got[1] + even
            sent_y.append(y_copies(j + 1))
            for copy in sent_y[j + 1]:
                copy.start()
            sent_x.append(x_copies(j + 1))
            for copy in sent_x[j + 1]:
                copy.start()

    part[...] = jnp.concatenate(
        [jnp.sum(t, axis=0, keepdims=True) for t in moments]
        + [jnp.zeros((8 - 2 * ITERS, Y), F32)],
        axis=0,
    )

    def total_over(axis, me, size, source, slots, send_sem, recv_sem):
        copies = []
        for d in range(1, size):
            copies.append(
                pltpu.make_async_remote_copy(
                    src_ref=source, dst_ref=slots.at[d - 1],
                    send_sem=send_sem.at[d - 1], recv_sem=recv_sem.at[d - 1],
                    device_id={axis: lax.rem(me + d, size)}, device_id_type=MESH,
                )
            )
            copies[-1].start()
        total = source[...]
        for d in range(1, size):
            copies[d - 1].wait()
            total = total + slots[d - 1]
        return total

    mid[...] = total_over("gx", ix, sx, part, slots_x, ax_s, ax_r)
    total = total_over("gy", iy, sy, mid, slots_y, ay_s, ay_r)
    summed = jnp.broadcast_to(jnp.sum(total, axis=1, keepdims=True), (8, Y))
    press, resid = coefficients([summed[i:i + 1] for i in range(2 * ITERS)])

    coef[...] = jnp.concatenate(press + resid + [jnp.zeros((1, Y), F32)], axis=0)


def combine(bs, ws, coef, p_hbm, r_hbm, p_buf, r_buf, sem):
    K, X, Y = p_hbm.shape
    c = [coef[i:i + 1] for i in range(2 * ITERS + 1)]
    copies = []
    for x in range(X):
        p = c[0] * ws[0, x + 1]
        r = c[ITERS] * bs[0, x]
        for j in range(1, ITERS):
            p = p + c[j] * ws[j, x + 1]
        for j in range(1, ITERS + 1):
            r = r + c[ITERS + j] * bs[j, x]
        p_buf[x] = p
        r_buf[x] = r
        copies.append(pltpu.make_async_copy(p_buf.at[x], p_hbm.at[:, x, :], sem.at[0, x]))
        copies.append(pltpu.make_async_copy(r_buf.at[x], r_hbm.at[:, x, :], sem.at[1, x]))
        copies[-2].start()
        copies[-1].start()
    for copy in copies:
        copy.wait()


def on_device(sx, sy, source_heat, horiz_coef, face_coef, column_inverse):
    K, X, Y = source_heat.shape
    KG = K // (Y // (2 * X))
    hbm = pl.BlockSpec(memory_space=pltpu.HBM)
    vmem = pl.BlockSpec(memory_space=pltpu.VMEM)
    dma = pltpu.SemaphoreType.DMA
    bs, ws, coef = pl.pallas_call(
        functools.partial(kernel, sx, sy),
        out_shape=(
            jax.ShapeDtypeStruct((ITERS + 1, X, K, Y), F32),
            jax.ShapeDtypeStruct((ITERS, X + 2, K, Y), F32),
            jax.ShapeDtypeStruct((8, Y), F32),
        ),
        in_specs=[hbm, hbm, hbm],
        out_specs=(vmem, vmem, vmem),
        scratch_shapes=[
            pltpu.VMEM((1, K), F32),
            pltpu.VMEM((K, K), F32),
            pltpu.VMEM((K, 3 * K), BF16),
            pltpu.VMEM((3 * ITERS, KG, Y), F32),
            pltpu.VMEM((ITERS, KG, Y), F32),
            pltpu.VMEM((8, Y), F32),
            pltpu.VMEM((sx - 1, 8, Y), F32),
            pltpu.VMEM((8, Y), F32),
            pltpu.VMEM((sy - 1, 8, Y), F32),
            dma((X,)),
            dma((2,)),
            dma((ITERS, 2)),
            dma((ITERS, 2)),
            dma((ITERS, 2)),
            dma((ITERS, 2)),
            dma((sx - 1,)),
            dma((sx - 1,)),
            dma((sy - 1,)),
            dma((sy - 1,)),
        ],
        compiler_params=pltpu.CompilerParams(
            collective_id=0, has_side_effects=True, vmem_limit_bytes=24 << 20
        ),
        name="pcg",
    )(
        pltpu.with_memory_space_constraint(source_heat, pltpu.HBM),
        pltpu.with_memory_space_constraint(horiz_coef.reshape(1, K), pltpu.HBM),
        pltpu.with_memory_space_constraint(column_inverse, pltpu.HBM),
    )
    out = jax.ShapeDtypeStruct((K, X, Y), F32)
    return pl.pallas_call(
        combine,
        out_shape=(out, out),
        in_specs=[vmem, vmem, vmem],
        out_specs=(hbm, hbm),
        scratch_shapes=[
            pltpu.VMEM((X, K, Y), F32),
            pltpu.VMEM((X, K, Y), F32),
            dma((2, X)),
        ],
        compiler_params=pltpu.CompilerParams(vmem_limit_bytes=24 << 20),
        name="combine",
    )(bs, ws, coef)


def solution(mesh):
    in_specs = (P(None, "gx", "gy"), P(), P(), P())
    out_specs = (P(None, "gx", "gy"), P(None, "gx", "gy"))
    body = functools.partial(on_device, mesh.shape["gx"], mesh.shape["gy"])
    return jax.shard_map(
        body, mesh=mesh, in_specs=in_specs, out_specs=out_specs, check_vma=False
    )
```

```python
import functools

import jax
import jax.numpy as jnp
from jax import lax
from jax.experimental import pallas as pl
from jax.experimental.pallas import tpu as pltpu
from jax.sharding import PartitionSpec as P

ITERS = 3
MESH = pl.DeviceIdType.MESH
F32 = jnp.float32
BF16 = jnp.bfloat16


def split2(v):
    high = v.astype(BF16)
    low = (v - high.astype(F32)).astype(BF16)
    return high, low


def folded(v):
    return jnp.sum(v.reshape(v.shape[0] // 8, 8, v.shape[1]), axis=0)


def coefficients(m):
    press = []
    inner = m[0]
    one = jnp.ones_like(m[0])
    rho, delta = [one], [one]
    for it in range(ITERS):
        n = len(delta)
        dad = 0.0
        for i in range(n):
            for j in range(n):
                dad = dad + delta[i] * delta[j] * (m[i + j] - m[i + j + 1])
        step = inner / dad
        press = [
            (press[i] if i < len(press) else 0.0) + step * delta[i] for i in range(n)
        ]
        image = [
            (delta[i] if i < n else 0.0) - (delta[i - 1] if i else 0.0)
            for i in range(n + 1)
        ]
        rho = [(rho[i] if i < n else 0.0) - step * image[i] for i in range(n + 1)]
        if it + 1 < ITERS:
            inner_next = 0.0
            for i in range(n + 1):
                for j in range(n + 1):
                    inner_next = inner_next + rho[i] * rho[j] * m[i + j]
            ratio = inner_next / inner
            delta = [
                rho[i] + (ratio * delta[i] if i < n else 0.0) for i in range(n + 1)
            ]
            inner = inner_next
    resid = (
        [1.0 - press[0]]
        + [press[i - 1] - press[i] for i in range(1, ITERS)]
        + [press[ITERS - 1]]
    )
    return press, resid


def kernel(
    sx, sy, b_hbm, h_hbm, m_hbm, bs, ws, coef,
    h_ref, m_ref, mcat, pack, halo, part, slots,
    load_sem, small_sem, xs_sem, xr_sem, ys_sem, yr_sem,
    all_s, all_r,
):
    K, X, Y = b_hbm.shape
    G = Y // (2 * X)
    KG = K // G
    ix, iy = lax.axis_index("gx"), lax.axis_index("gy")
    xn, xp = lax.rem(ix + 1, sx), lax.rem(ix + sx - 1, sx)
    yn, yp = lax.rem(iy + 1, sy), lax.rem(iy + sy - 1, sy)

    barrier = pltpu.get_barrier_semaphore()
    peers = [
        (lax.rem(ix + dx, sx), lax.rem(iy + dy, sy))
        for dx in range(sx) for dy in range(sy) if dx or dy
    ]
    for peer in peers:
        pl.semaphore_signal(barrier, inc=1, device_id=peer, device_id_type=MESH)

    order = [0, X - 1] + list(range(1, X - 1))
    loads = {
        x: pltpu.make_async_copy(b_hbm.at[:, x, :], bs.at[0, x], load_sem.at[x])
        for x in order
    }
    load_h = pltpu.make_async_copy(h_hbm, h_ref, small_sem.at[0])
    load_m = pltpu.make_async_copy(m_hbm, m_ref, small_sem.at[1])
    load_m.start()
    load_h.start()
    for x in order:
        loads[x].start()
    load_m.wait()
    load_h.wait()

    m1, m2 = split2(m_ref[...])
    mcat[...] = jnp.concatenate([m1.astype(F32), m1.astype(F32), m2.astype(F32)], axis=1).astype(BF16)
    rows = lax.broadcasted_iota(jnp.int32, (K, K), 0)
    cols = lax.broadcasted_iota(jnp.int32, (K, K), 1)
    h_col = jnp.sum(jnp.where(rows == cols, h_ref[...], 0.0), axis=1, keepdims=True)
    h_b = jnp.broadcast_to(h_col, (K, Y))
    lane = lax.broadcasted_iota(jnp.int32, (KG, Y), 1)
    lane_full = lax.broadcasted_iota(jnp.int32, (K, Y), 1)

    def matmul(v0, v1):
        h0, l0 = split2(v0)
        h1, l1 = split2(v1)
        high = jnp.concatenate([h0, h1], axis=1)
        low = jnp.concatenate([l0, l1], axis=1)
        stacked = jnp.concatenate([high, low, high], axis=0)
        out = jnp.dot(mcat[...], stacked, preferred_element_type=F32)
        return out[:, :Y], out[:, Y:]

    def packed(j, x, v):
        acc = pack[j]
        for g in range(G):
            shift = lax.rem(2 * X * g + 2 * x, Y)
            turned = pltpu.roll(v[g * KG:(g + 1) * KG], shift, 1)
            here = (lane == shift) | (lane == lax.rem(shift + Y - 1, Y))
            acc = jnp.where(here, turned, acc)
        pack[j] = acc

    def turned_sum(v):
        return pltpu.roll(v, 1, 1) + pltpu.roll(v, Y - 1, 1)

    def periodic(j, x):
        bs[j + 1, x] = ws[j, x] + ws[j, x + 2] + turned_sum(ws[j, x + 1])

    edge = (lane_full == 0) | (lane_full == Y - 1)

    def beside(j, x):
        c = halo[j]
        turned = jnp.concatenate(
            [
                pltpu.roll(c, lax.rem(2 * Y - 2 * X * g - 2 * x, Y), 1)
                for g in range(G)
            ],
            axis=0,
        )
        return ws[j, x + 1], bs[j + 1, x] + jnp.where(edge, turned, 0.0)

    def through_m(j, x0, x1, v0, v1):
        w0, w1 = matmul(v0, v1)
        ws[j, x0 + 1] = w0
        ws[j, x1 + 1] = w1
        packed(j, x0, w0)
        packed(j, x1, w1)
        return folded(v0 * w0 + v1 * w1)

    def level(j, x0, x1):
        w0, s0 = beside(j, x0)
        w1, s1 = beside(j, x1)
        b0, b1 = h_b * s0, h_b * s1
        bs[j + 1, x0] = b0
        bs[j + 1, x1] = b1
        odd = folded(b0 * w0 + b1 * w1)
        even = None
        if j + 1 < ITERS:
            even = through_m(j + 1, x0, x1, b0, b1)
        return odd, even

    def x_copies(j):
        return (
            pltpu.make_async_remote_copy(
                src_ref=ws.at[j, X], dst_ref=ws.at[j, 0],
                send_sem=xs_sem.at[j, 0], recv_sem=xr_sem.at[j, 0],
                device_id={"gx": xn}, device_id_type=MESH,
            ),
            pltpu.make_async_remote_copy(
                src_ref=ws.at[j, 1], dst_ref=ws.at[j, X + 1],
                send_sem=xs_sem.at[j, 1], recv_sem=xr_sem.at[j, 1],
                device_id={"gx": xp}, device_id_type=MESH,
            ),
        )

    def y_copies(j):
        return (
            pltpu.make_async_remote_copy(
                src_ref=pack.at[j], dst_ref=pack.at[ITERS + j],
                send_sem=ys_sem.at[j, 0], recv_sem=yr_sem.at[j, 0],
                device_id={"gy": yn}, device_id_type=MESH,
            ),
            pltpu.make_async_remote_copy(
                src_ref=pack.at[j], dst_ref=pack.at[2 * ITERS + j],
                send_sem=ys_sem.at[j, 1], recv_sem=yr_sem.at[j, 1],
                device_id={"gy": yp}, device_id_type=MESH,
            ),
        )

    zero = jnp.zeros((8, Y), F32)
    moments = [zero] * (2 * ITERS)
    for j in range(ITERS):
        pack[j] = jnp.zeros((KG, Y), F32)

    loads[0].wait()
    loads[X - 1].wait()
    even = through_m(0, 0, X - 1, bs[0, 0], bs[0, X - 1])

    def first(i, acc):
        x0 = 2 * i + 1
        for x in (x0, x0 + 1):
            pltpu.make_async_copy(b_hbm.at[:, x, :], bs.at[0, x], load_sem.at[x]).wait()
        return acc + through_m(0, x0, x0 + 1, bs[0, x0], bs[0, x0 + 1])

    moments[0] = lax.fori_loop(0, (X - 2) // 2, first, even, unroll=True)
    pl.semaphore_wait(barrier, sx * sy - 1)
    sent_y = [y_copies(0)]
    for copy in sent_y[0]:
        copy.start()
    sent_x = [x_copies(0)]
    for copy in sent_x[0]:
        copy.start()

    def finish_halo(j):
        for copy in sent_y[j]:
            copy.wait()
        mine = pack[j]
        from_left, from_right = pack[ITERS + j] - mine, pack[2 * ITERS + j] - mine
        halo[j] = jnp.where(
            lane % 2 == 0, pltpu.roll(from_left, 1, 1), pltpu.roll(from_right, Y - 1, 1)
        )

    pairs = (X - 2) // 2
    last = ITERS - 1
    for j in range(last):
        def ahead(i, carry):
            periodic(j, 2 * i + 1)
            periodic(j, 2 * i + 2)
            return carry

        lax.fori_loop(0, pairs, ahead, 0, unroll=True)
        finish_halo(j)

        def inside(i, acc):
            x0 = 2 * i + 1
            odd, even = level(j, x0, x0 + 1)
            return (acc[0] + odd, acc[1] + even)

        got = lax.fori_loop(0, pairs, inside, (zero, zero), unroll=True)
        for copy in sent_x[j]:
            copy.wait()
        periodic(j, 0)
        periodic(j, X - 1)
        odd, even = level(j, 0, X - 1)
        moments[2 * j + 1] = got[0] + odd
        moments[2 * j + 2] = got[1] + even
        sent_y.append(y_copies(j + 1))
        for copy in sent_y[j + 1]:
            copy.start()
        sent_x.append(x_copies(j + 1))
        for copy in sent_x[j + 1]:
            copy.start()

    def last_row(x):
        v = ws[last, x + 1]
        total = ws[last, x] + ws[last, x + 2] + turned_sum(v)
        bs[last + 1, x] = total
        return folded(h_b * total * v)

    def last_ahead(i, acc):
        return acc + last_row(2 * i + 1) + last_row(2 * i + 2)

    odd = lax.fori_loop(0, pairs, last_ahead, zero, unroll=True)
    group = lax.rem(lane + 1, Y) // (2 * X)
    h_packed = h_b[:KG]
    for g in range(1, G):
        h_packed = jnp.where(group == g, h_b[g * KG:(g + 1) * KG], h_packed)
    for copy in sent_x[last]:
        copy.wait()
    odd = odd + last_row(0) + last_row(X - 1)
    finish_halo(last)
    moments[2 * last + 1] = odd + folded(pack[last] * halo[last] * h_packed)

    eight = (8, Y)
    diagonal = lax.broadcasted_iota(jnp.int32, eight, 0) == lax.broadcasted_iota(
        jnp.int32, eight, 1
    )
    sums = jnp.concatenate(
        [jnp.sum(t, axis=0, keepdims=True) for t in moments]
        + [jnp.zeros((8 - 2 * ITERS, Y), F32)],
        axis=0,
    )
    sums = jnp.sum(sums, axis=1, keepdims=True)
    part[...] = jnp.sum(jnp.where(diagonal, sums, 0.0), axis=0, keepdims=True)
    copies = [
        pltpu.make_async_remote_copy(
            src_ref=part, dst_ref=slots.at[d],
            send_sem=all_s.at[d], recv_sem=all_r.at[d],
            device_id=peer, device_id_type=MESH,
        )
        for d, peer in enumerate(peers)
    ]
    for copy in copies:
        copy.start()

    def corrected(i, carry):
        for x in (2 * i, 2 * i + 1):
            bs[last + 1, x] = h_b * beside(last, x)[1]
        return carry

    lax.fori_loop(0, X // 2, corrected, 0, unroll=True)
    for copy in copies:
        copy.wait()
    total = part[...] + jnp.sum(slots[...], axis=0)
    summed = jnp.sum(jnp.where(diagonal, total, 0.0), axis=1, keepdims=True)
    summed = jnp.broadcast_to(summed, eight)
    press, resid = coefficients([summed[i:i + 1] for i in range(2 * ITERS)])
    coef[...] = jnp.concatenate(press + resid + [jnp.zeros((1, Y), F32)], axis=0)


def combine(bs, ws, coef, p_hbm, r_hbm, p_buf, r_buf, sem):
    K, X, Y = p_hbm.shape
    c = [coef[i:i + 1] for i in range(2 * ITERS + 1)]
    copies = []
    for x in range(X):
        p = c[0] * ws[0, x + 1]
        r = c[ITERS] * bs[0, x]
        for j in range(1, ITERS):
            p = p + c[j] * ws[j, x + 1]
        for j in range(1, ITERS + 1):
            r = r + c[ITERS + j] * bs[j, x]
        p_buf[x] = p
        r_buf[x] = r
        copies.append(pltpu.make_async_copy(p_buf.at[x], p_hbm.at[:, x, :], sem.at[0, x]))
        copies.append(pltpu.make_async_copy(r_buf.at[x], r_hbm.at[:, x, :], sem.at[1, x]))
        copies[-2].start()
        copies[-1].start()
    for copy in copies:
        copy.wait()


def on_device(sx, sy, source_heat, horiz_coef, face_coef, column_inverse):
    K, X, Y = source_heat.shape
    KG = K // (Y // (2 * X))
    hbm = pl.BlockSpec(memory_space=pltpu.HBM)
    vmem = pl.BlockSpec(memory_space=pltpu.VMEM)
    dma = pltpu.SemaphoreType.DMA
    bs, ws, coef = pl.pallas_call(
        functools.partial(kernel, sx, sy),
        out_shape=(
            jax.ShapeDtypeStruct((ITERS + 1, X, K, Y), F32),
            jax.ShapeDtypeStruct((ITERS, X + 2, K, Y), F32),
            jax.ShapeDtypeStruct((8, Y), F32),
        ),
        in_specs=[hbm, hbm, hbm],
        out_specs=(vmem, vmem, vmem),
        scratch_shapes=[
            pltpu.VMEM((1, K), F32),
            pltpu.VMEM((K, K), F32),
            pltpu.VMEM((K, 3 * K), BF16),
            pltpu.VMEM((3 * ITERS, KG, Y), F32),
            pltpu.VMEM((ITERS, KG, Y), F32),
            pltpu.VMEM((1, Y), F32),
            pltpu.VMEM((sx * sy - 1, 1, Y), F32),
            dma((X,)),
            dma((2,)),
            dma((ITERS, 2)),
            dma((ITERS, 2)),
            dma((ITERS, 2)),
            dma((ITERS, 2)),
            dma((sx * sy - 1,)),
            dma((sx * sy - 1,)),
        ],
        compiler_params=pltpu.CompilerParams(
            collective_id=0, has_side_effects=True, vmem_limit_bytes=24 << 20
        ),
        name="pcg",
    )(
        pltpu.with_memory_space_constraint(source_heat, pltpu.HBM),
        pltpu.with_memory_space_constraint(horiz_coef.reshape(1, K), pltpu.HBM),
        pltpu.with_memory_space_constraint(column_inverse, pltpu.HBM),
    )
    out = jax.ShapeDtypeStruct((K, X, Y), F32)
    return pl.pallas_call(
        combine,
        out_shape=(out, out),
        in_specs=[vmem, vmem, vmem],
        out_specs=(hbm, hbm),
        scratch_shapes=[
            pltpu.VMEM((X, K, Y), F32),
            pltpu.VMEM((X, K, Y), F32),
            dma((2, X)),
        ],
        compiler_params=pltpu.CompilerParams(vmem_limit_bytes=24 << 20),
        name="combine",
    )(bs, ws, coef)


def solution(mesh):
    in_specs = (P(None, "gx", "gy"), P(), P(), P())
    out_specs = (P(None, "gx", "gy"), P(None, "gx", "gy"))
    body = functools.partial(on_device, mesh.shape["gx"], mesh.shape["gy"])
    return jax.shard_map(
        body, mesh=mesh, in_specs=in_specs, out_specs=out_specs, check_vma=False
    )
```

```python
import functools

import jax
import jax.numpy as jnp
from jax import lax
from jax.experimental import pallas as pl
from jax.experimental.pallas import tpu as pltpu
from jax.sharding import PartitionSpec as P

ITERS = 3
MESH = pl.DeviceIdType.MESH
F32 = jnp.float32
BF16 = jnp.bfloat16


def split2(v):
    high = v.astype(BF16)
    low = (v - high.astype(F32)).astype(BF16)
    return high, low


def folded(v):
    return jnp.sum(v.reshape(v.shape[0] // 8, 8, v.shape[1]), axis=0)


def coefficients(m):
    press = []
    inner = m[0]
    one = jnp.ones_like(m[0])
    rho, delta = [one], [one]
    for it in range(ITERS):
        n = len(delta)
        dad = 0.0
        for i in range(n):
            for j in range(n):
                dad = dad + delta[i] * delta[j] * (m[i + j] - m[i + j + 1])
        step = inner / dad
        press = [
            (press[i] if i < len(press) else 0.0) + step * delta[i] for i in range(n)
        ]
        image = [
            (delta[i] if i < n else 0.0) - (delta[i - 1] if i else 0.0)
            for i in range(n + 1)
        ]
        rho = [(rho[i] if i < n else 0.0) - step * image[i] for i in range(n + 1)]
        if it + 1 < ITERS:
            inner_next = 0.0
            for i in range(n + 1):
                for j in range(n + 1):
                    inner_next = inner_next + rho[i] * rho[j] * m[i + j]
            ratio = inner_next / inner
            delta = [
                rho[i] + (ratio * delta[i] if i < n else 0.0) for i in range(n + 1)
            ]
            inner = inner_next
    resid = (
        [1.0 - press[0]]
        + [press[i - 1] - press[i] for i in range(1, ITERS)]
        + [press[ITERS - 1]]
    )
    return press, resid


def kernel(
    sx, sy, b_hbm, h_hbm, m_hbm, bs, ws, coef,
    h_ref, m_ref, mcat, pack, halo, h_full, part, slots,
    load_sem, small_sem, xs_sem, xr_sem, ys_sem, yr_sem,
    all_s, all_r,
):
    K, X, Y = b_hbm.shape
    G = Y // (2 * X)
    KG = K // G
    ix, iy = lax.axis_index("gx"), lax.axis_index("gy")
    xn, xp = lax.rem(ix + 1, sx), lax.rem(ix + sx - 1, sx)
    yn, yp = lax.rem(iy + 1, sy), lax.rem(iy + sy - 1, sy)

    barrier = pltpu.get_barrier_semaphore()
    peers = [
        (lax.rem(ix + dx, sx), lax.rem(iy + dy, sy))
        for dx in range(sx) for dy in range(sy) if dx or dy
    ]
    for peer in peers:
        pl.semaphore_signal(barrier, inc=1, device_id=peer, device_id_type=MESH)

    order = [0, X - 1] + list(range(1, X - 1))
    loads = {
        x: pltpu.make_async_copy(b_hbm.at[:, x, :], bs.at[0, x], load_sem.at[x])
        for x in order
    }
    load_h = pltpu.make_async_copy(h_hbm, h_ref, small_sem.at[0])
    load_m = pltpu.make_async_copy(m_hbm, m_ref, small_sem.at[1])
    load_m.start()
    load_h.start()
    for x in order:
        loads[x].start()
    load_m.wait()
    load_h.wait()

    m1, m2 = split2(m_ref[...])
    mcat[...] = jnp.concatenate([m1.astype(F32), m1.astype(F32), m2.astype(F32)], axis=1).astype(BF16)
    rows = lax.broadcasted_iota(jnp.int32, (K, K), 0)
    cols = lax.broadcasted_iota(jnp.int32, (K, K), 1)
    h_col = jnp.sum(jnp.where(rows == cols, h_ref[...], 0.0), axis=1, keepdims=True)
    h_full[...] = jnp.broadcast_to(h_col, (K, Y))
    lane = lax.broadcasted_iota(jnp.int32, (KG, Y), 1)
    lane_full = lax.broadcasted_iota(jnp.int32, (K, Y), 1)

    def matmul(v0, v1):
        h0, l0 = split2(v0)
        h1, l1 = split2(v1)
        high = jnp.concatenate([h0, h1], axis=1)
        low = jnp.concatenate([l0, l1], axis=1)
        stacked = jnp.concatenate([high, low, high], axis=0)
        out = jnp.dot(mcat[...], stacked, preferred_element_type=F32)
        return out[:, :Y], out[:, Y:]

    def packed(j, x, v):
        acc = pack[j]
        for g in range(G):
            shift = lax.rem(2 * X * g + 2 * x, Y)
            turned = pltpu.roll(v[g * KG:(g + 1) * KG], shift, 1)
            here = (lane == shift) | (lane == lax.rem(shift + Y - 1, Y))
            acc = jnp.where(here, turned, acc)
        pack[j] = acc

    def turned_sum(v):
        return pltpu.roll(v, 1, 1) + pltpu.roll(v, Y - 1, 1)

    def periodic(j, x):
        v = ws[j, x + 1]
        total = ws[j, x] + ws[j, x + 2] + turned_sum(v)
        bs[j + 1, x] = total
        return folded(bs[j, x] * v), folded(h_full[...] * total * v)

    def periodic_two(j, x0, x1, acc):
        even0, odd0 = periodic(j, x0)
        even1, odd1 = periodic(j, x1)
        return acc[0] + (even0 + even1), acc[1] + (odd0 + odd1)

    edge = (lane_full == 0) | (lane_full == Y - 1)

    def beside(j, x):
        c = halo[j]
        turned = jnp.concatenate(
            [
                pltpu.roll(c, lax.rem(2 * Y - 2 * X * g - 2 * x, Y), 1)
                for g in range(G)
            ],
            axis=0,
        )
        return ws[j, x + 1], bs[j + 1, x] + jnp.where(edge, turned, 0.0)

    def through_m(j, x0, x1, v0, v1):
        w0, w1 = matmul(v0, v1)
        ws[j, x0 + 1] = w0
        ws[j, x1 + 1] = w1
        packed(j, x0, w0)
        packed(j, x1, w1)

    def level(j, x0, x1):
        w0, s0 = beside(j, x0)
        w1, s1 = beside(j, x1)
        b0, b1 = h_full[...] * s0, h_full[...] * s1
        bs[j + 1, x0] = b0
        bs[j + 1, x1] = b1
        through_m(j + 1, x0, x1, b0, b1)

    def x_copies(j):
        return (
            pltpu.make_async_remote_copy(
                src_ref=ws.at[j, X], dst_ref=ws.at[j, 0],
                send_sem=xs_sem.at[j, 0], recv_sem=xr_sem.at[j, 0],
                device_id={"gx": xn}, device_id_type=MESH,
            ),
            pltpu.make_async_remote_copy(
                src_ref=ws.at[j, 1], dst_ref=ws.at[j, X + 1],
                send_sem=xs_sem.at[j, 1], recv_sem=xr_sem.at[j, 1],
                device_id={"gx": xp}, device_id_type=MESH,
            ),
        )

    def y_copies(j):
        return (
            pltpu.make_async_remote_copy(
                src_ref=pack.at[j], dst_ref=pack.at[ITERS + j],
                send_sem=ys_sem.at[j, 0], recv_sem=yr_sem.at[j, 0],
                device_id={"gy": yn}, device_id_type=MESH,
            ),
            pltpu.make_async_remote_copy(
                src_ref=pack.at[j], dst_ref=pack.at[2 * ITERS + j],
                send_sem=ys_sem.at[j, 1], recv_sem=yr_sem.at[j, 1],
                device_id={"gy": yp}, device_id_type=MESH,
            ),
        )

    zero = jnp.zeros((8, Y), F32)
    moments = [zero] * (2 * ITERS)
    for j in range(ITERS):
        pack[j] = jnp.zeros((KG, Y), F32)

    loads[0].wait()
    loads[X - 1].wait()
    through_m(0, 0, X - 1, bs[0, 0], bs[0, X - 1])

    def first(i, acc):
        x0 = 2 * i + 1
        for x in (x0, x0 + 1):
            pltpu.make_async_copy(b_hbm.at[:, x, :], bs.at[0, x], load_sem.at[x]).wait()
        through_m(0, x0, x0 + 1, bs[0, x0], bs[0, x0 + 1])
        return acc

    lax.fori_loop(0, (X - 2) // 2, first, 0, unroll=True)
    pl.semaphore_wait(barrier, sx * sy - 1)
    sent_y = [y_copies(0)]
    for copy in sent_y[0]:
        copy.start()
    sent_x = [x_copies(0)]
    for copy in sent_x[0]:
        copy.start()

    def finish_halo(j):
        for copy in sent_y[j]:
            copy.wait()
        mine = pack[j]
        from_left, from_right = pack[ITERS + j] - mine, pack[2 * ITERS + j] - mine
        halo[j] = jnp.where(
            lane % 2 == 0, pltpu.roll(from_left, 1, 1), pltpu.roll(from_right, Y - 1, 1)
        )

    pairs = (X - 2) // 2
    last = ITERS - 1
    group = lax.rem(lane + 1, Y) // (2 * X)
    h_packed = h_full[:KG]
    for g in range(1, G):
        h_packed = jnp.where(group == g, h_full[g * KG:(g + 1) * KG], h_packed)
    for j in range(ITERS):
        def ahead(i, acc):
            return periodic_two(j, 2 * i + 1, 2 * i + 2, acc)

        got = lax.fori_loop(0, pairs, ahead, (zero, zero), unroll=True)
        if j == last:
            for copy in sent_x[j]:
                copy.wait()
            got = periodic_two(j, 0, X - 1, got)
        finish_halo(j)
        if j < last:
            def inside(i, carry):
                level(j, 2 * i + 1, 2 * i + 2)
                return carry

            lax.fori_loop(0, pairs, inside, 0, unroll=True)
            for copy in sent_x[j]:
                copy.wait()
            got = periodic_two(j, 0, X - 1, got)
            level(j, 0, X - 1)
            sent_y.append(y_copies(j + 1))
            for copy in sent_y[j + 1]:
                copy.start()
            sent_x.append(x_copies(j + 1))
            for copy in sent_x[j + 1]:
                copy.start()
        moments[2 * j] = got[0]
        moments[2 * j + 1] = got[1] + folded(pack[j] * halo[j] * h_packed)

    eight = (8, Y)
    diagonal = lax.broadcasted_iota(jnp.int32, eight, 0) == lax.broadcasted_iota(
        jnp.int32, eight, 1
    )
    sums = jnp.concatenate(
        [jnp.sum(t, axis=0, keepdims=True) for t in moments]
        + [jnp.zeros((8 - 2 * ITERS, Y), F32)],
        axis=0,
    )
    sums = jnp.sum(sums, axis=1, keepdims=True)
    part[...] = jnp.sum(jnp.where(diagonal, sums, 0.0), axis=0, keepdims=True)
    copies = [
        pltpu.make_async_remote_copy(
            src_ref=part, dst_ref=slots.at[d],
            send_sem=all_s.at[d], recv_sem=all_r.at[d],
            device_id=peer, device_id_type=MESH,
        )
        for d, peer in enumerate(peers)
    ]
    for copy in copies:
        copy.start()

    def corrected(i, carry):
        for x in (2 * i, 2 * i + 1):
            bs[last + 1, x] = h_full[...] * beside(last, x)[1]
        return carry

    lax.fori_loop(0, X // 2, corrected, 0, unroll=True)
    for copy in copies:
        copy.wait()
    total = part[...] + jnp.sum(slots[...], axis=0)
    summed = jnp.sum(jnp.where(diagonal, total, 0.0), axis=1, keepdims=True)
    summed = jnp.broadcast_to(summed, eight)
    press, resid = coefficients([summed[i:i + 1] for i in range(2 * ITERS)])
    coef[...] = jnp.concatenate(press + resid + [jnp.zeros((1, Y), F32)], axis=0)


def combine(bs, ws, coef, p_hbm, r_hbm, p_buf, r_buf, sem):
    K, X, Y = p_hbm.shape
    c = [coef[i:i + 1] for i in range(2 * ITERS + 1)]
    copies = []
    for x in range(X):
        p = c[0] * ws[0, x + 1]
        r = c[ITERS] * bs[0, x]
        for j in range(1, ITERS):
            p = p + c[j] * ws[j, x + 1]
        for j in range(1, ITERS + 1):
            r = r + c[ITERS + j] * bs[j, x]
        p_buf[x] = p
        r_buf[x] = r
        copies.append(pltpu.make_async_copy(p_buf.at[x], p_hbm.at[:, x, :], sem.at[0, x]))
        copies.append(pltpu.make_async_copy(r_buf.at[x], r_hbm.at[:, x, :], sem.at[1, x]))
        copies[-2].start()
        copies[-1].start()
    for copy in copies:
        copy.wait()


def on_device(sx, sy, source_heat, horiz_coef, face_coef, column_inverse):
    K, X, Y = source_heat.shape
    KG = K // (Y // (2 * X))
    hbm = pl.BlockSpec(memory_space=pltpu.HBM)
    vmem = pl.BlockSpec(memory_space=pltpu.VMEM)
    dma = pltpu.SemaphoreType.DMA
    bs, ws, coef = pl.pallas_call(
        functools.partial(kernel, sx, sy),
        out_shape=(
            jax.ShapeDtypeStruct((ITERS + 1, X, K, Y), F32),
            jax.ShapeDtypeStruct((ITERS, X + 2, K, Y), F32),
            jax.ShapeDtypeStruct((8, Y), F32),
        ),
        in_specs=[hbm, hbm, hbm],
        out_specs=(vmem, vmem, vmem),
        scratch_shapes=[
            pltpu.VMEM((1, K), F32),
            pltpu.VMEM((K, K), F32),
            pltpu.VMEM((K, 3 * K), BF16),
            pltpu.VMEM((3 * ITERS, KG, Y), F32),
            pltpu.VMEM((ITERS, KG, Y), F32),
            pltpu.VMEM((K, Y), F32),
            pltpu.VMEM((1, Y), F32),
            pltpu.VMEM((sx * sy - 1, 1, Y), F32),
            dma((X,)),
            dma((2,)),
            dma((ITERS, 2)),
            dma((ITERS, 2)),
            dma((ITERS, 2)),
            dma((ITERS, 2)),
            dma((sx * sy - 1,)),
            dma((sx * sy - 1,)),
        ],
        compiler_params=pltpu.CompilerParams(
            collective_id=0, has_side_effects=True, vmem_limit_bytes=24 << 20
        ),
        name="pcg",
    )(
        pltpu.with_memory_space_constraint(source_heat, pltpu.HBM),
        pltpu.with_memory_space_constraint(horiz_coef.reshape(1, K), pltpu.HBM),
        pltpu.with_memory_space_constraint(column_inverse, pltpu.HBM),
    )
    out = jax.ShapeDtypeStruct((K, X, Y), F32)
    return pl.pallas_call(
        combine,
        out_shape=(out, out),
        in_specs=[vmem, vmem, vmem],
        out_specs=(hbm, hbm),
        scratch_shapes=[
            pltpu.VMEM((X, K, Y), F32),
            pltpu.VMEM((X, K, Y), F32),
            dma((2, X)),
        ],
        compiler_params=pltpu.CompilerParams(vmem_limit_bytes=24 << 20),
        name="combine",
    )(bs, ws, coef)


def solution(mesh):
    in_specs = (P(None, "gx", "gy"), P(), P(), P())
    out_specs = (P(None, "gx", "gy"), P(None, "gx", "gy"))
    body = functools.partial(on_device, mesh.shape["gx"], mesh.shape["gy"])
    return jax.shard_map(
        body, mesh=mesh, in_specs=in_specs, out_specs=out_specs, check_vma=False
    )
```
